1024 devices in a mesh: pipe: 16 (over z), expert: 16 (over x, y_hi), tensor: 4 (over y_lo, core).
Axes of the slice: x: 4, y: 8 (y_hi: 4, y_lo: 2; y = y_hi * 2 + y_lo), z: 16, core: 2. Of those that a mesh axis runs over, the one named last changes fastest.
Arguments:
- acts: bfloat16 [16, 16, 256, 1792], P('pipe', 'expert'), may hold values from -6 to 6
- hidden_grad: bfloat16 [16, 8, 256, 1024], P('pipe', None, None, 'tensor'), may hold values from -0.5 to 0.5
- counts: int32 [16, 8, 2], P('pipe'), may hold values from 32 to 128, as said below
- momentum: bfloat16 [16, 16, 1792, 1024], P('pipe', 'expert', 'tensor'), may hold values from -6 to 6
- act_grad: bfloat16 [16, 1024, 7168], P('pipe', 'expert', 'tensor'), may hold values from -6 to 6
Outputs:
- new_momentum: bfloat16 [16, 16, 1792, 1024], P('pipe', 'expert', 'tensor')
- gram_rows: float32 [16, 16, 256, 1024], P('pipe', 'expert', 'tensor')
- received: bfloat16 [16, 1024, 7168], P('pipe', 'expert', 'tensor')
The draws below stay inside these ranges and needn't reach their ends.
Inputs may be any that keep to these rules, and one draw needn't show every extreme that they name: `counts`: in every section and expert, at least one micro-batch fills its block.
All inputs are finite; a program needn't handle non-finite values.
Results may differ from the reference program's by a relative error of at most 0.0065.
Values may be sent and summed in bfloat16 or wider, within the bound.
No kernel may reach another device: no remote copies, remote signals or barrier semaphores. Data moves between devices by JAX's collectives and lax.ppermute only.
A program may use at most 32 MiB of HBM per device.

```python
import jax
import jax.numpy as jnp
from jax import lax

D = 3584
H = 1024
DM = 7168
PANEL = 512
BLOCK = 128
MICRO = 2
ROWS = 256
SECTIONS = 16
EXPERTS = 8
SLOTS = 16
TOK = 1024
N_TENSOR = 4


def draw_counts(key, part):
    first_key, second_key = jax.random.split(key)
    shape_all = (SECTIONS, EXPERTS, MICRO)
    base_counts = jax.random.randint(first_key, shape_all, BLOCK // 4, BLOCK + 1)
    full_slot = jax.random.randint(second_key, (SECTIONS, EXPERTS, 1), 0, MICRO)
    slot_index = lax.broadcasted_iota(jnp.int32, shape_all, 2)
    return jnp.where(slot_index == full_slot, BLOCK, base_counts).astype(jnp.int32)


def block_scale(stream_key, dims, shards, low, high):
    def one(axis_at, blocks):
        steps = jax.random.uniform(jax.random.fold_in(jax.random.fold_in(stream_key, 6), axis_at), (blocks,), jnp.float32, low / len(shards), high / len(shards))
        return jnp.repeat(jnp.exp(steps), dims[axis_at] // blocks).reshape((-1,) + (1,) * (len(dims) - axis_at - 1))

    loudness = one(*shards[0])
    for cut in shards[1:]:
        loudness = loudness * one(*cut)
    return loudness


def centred(key, dims, width, most, pieces=(), held_as=jnp.bfloat16):
    gain = block_scale(key, dims, pieces, -0.22, 0.18) if pieces else 1.0
    array = jax.random.normal(key, dims, jnp.float32) * width * gain
    return jnp.minimum(jnp.maximum(array, -most), most).astype(held_as)


def setup_inputs(seed: int = 0) -> dict:
    seeds = jax.random.split(jax.random.key(seed), 6)
    return {
        "acts": centred(seeds[0], (SECTIONS, SLOTS, ROWS, D // 2), 1.0, 6.0, ((0, 16), (1, 16))),
        "hidden_grad": centred(seeds[1], (SECTIONS, EXPERTS, ROWS, H), 0.08, 0.5, ((0, 16), (3, 4))),
        "counts": draw_counts(jax.random.fold_in(seeds[5], 71), 0),
        "momentum": centred(seeds[3], (SECTIONS, SLOTS, D // 2, H), 1.0, 6.0, ((0, 16), (1, 16), (2, 4))),
        "act_grad": centred(seeds[4], (SECTIONS, TOK, DM), 1.0, 6.0, ((0, 16), (1, 16), (2, 4))),
    }


def contract(left, right):
    return lax.dot_general(left, right, (((0,), (0,)), ((), ())), preferred_element_type=jnp.float32)


def one_expert(inputs):
    features, gradients, counts_row, moment = inputs
    live_rows = (counts_row[:, None] > jnp.arange(BLOCK, dtype=jnp.int32)[None, :]).reshape(-1)
    masked = jnp.where(live_rows[:, None], gradients, jnp.zeros_like(gradients))
    grad_w = contract(features, masked).astype(jnp.bfloat16)
    new_full = (0.9 * moment.astype(jnp.float32) + grad_w.astype(jnp.float32)).astype(jnp.bfloat16)
    gram_full = contract(new_full[:, :PANEL], new_full) / D
    quarter = PANEL // (2 * N_TENSOR)
    gram_split = gram_full.reshape(N_TENSOR, 2, quarter, H).transpose(1, 0, 2, 3).reshape(2, PANEL // 2, H)
    return new_full, gram_split


def reference(acts, hidden_grad, counts, momentum, act_grad):
    total = SECTIONS * EXPERTS
    features = acts.reshape(SECTIONS, EXPERTS, 2, ROWS, D // 2).transpose(0, 1, 3, 2, 4).reshape(total, ROWS, D)
    moments = momentum.reshape(total, D, H)
    new_full, gram_split = lax.map(one_expert, (features, hidden_grad.reshape(total, ROWS, H), counts.reshape(total, MICRO), moments))
    new_momentum = new_full.reshape(SECTIONS, SLOTS, D // 2, H)
    gram_rows = gram_split.reshape(SECTIONS, SLOTS, PANEL // 2, H)
    received = jnp.concatenate([act_grad[1:], jnp.zeros_like(act_grad[:1])], axis=0)
    return (new_momentum, gram_rows, received)
```

```python
import jax
import jax.numpy as jnp
from jax import lax
from jax.experimental import pallas as pl
from jax.experimental.pallas import tpu as pltpu
from jax.sharding import PartitionSpec as P

D = 3584
PANEL = 512
Y_HI = 4
DECAY = 0.9


def prepare(acts_ref, counts_ref, xt_ref, window, sem):
    width = window.shape[1]
    pair = lax.axis_index("expert") // 2
    start = pl.multiple_of(lax.axis_index("tensor") // 2 * width, 128)
    fetch = pltpu.make_async_copy(acts_ref.at[0, 0, :, pl.ds(start, width)], window, sem)
    fetch.start()
    fetch.wait()
    rows = window.shape[0]
    micro = counts_ref.shape[2]
    block = rows // micro
    row = lax.broadcasted_iota(jnp.int32, (block, width), 0)
    for m in range(micro):
        part = window[m * block : (m + 1) * block, :]
        part = jnp.where(row < counts_ref[0, pair, m], part, jnp.zeros_like(part))
        xt_ref[:, m * block : (m + 1) * block] = part.T


def main(xt_ref, h0, h1, h2, h3, own_ref, mate_ref, new_ref, keep_ref, near_ref, side_ref, far_ref, full, gram):
    t = lax.axis_index("tensor")
    half = lax.axis_index("expert") % 2
    core, chip = t % 2, t // 2
    rows = own_ref.shape[0]
    for k, piece in enumerate((h0, h1, h2, h3)):
        width = piece.shape[1]
        col = pl.multiple_of(jnp.bitwise_xor(t, k) * width, 128)
        for i, (who, moment) in enumerate(((core, own_ref), (1 - core, mate_ref))):
            x = xt_ref[pl.ds(pl.multiple_of(who * rows, 64), rows), :]
            grad = jnp.dot(x, piece[...], preferred_element_type=jnp.float32).astype(jnp.bfloat16)
            new = DECAY * moment[:, pl.ds(col, width)].astype(jnp.float32) + grad.astype(jnp.float32)
            new = new.astype(jnp.bfloat16)
            full[i * rows : (i + 1) * rows, pl.ds(col, width)] = new
            if i == 0:
                new_ref[:, pl.ds(col, width)] = new
    share = gram.shape[0] // 2
    for i in range(2):
        left = full[:, pl.ds(pl.multiple_of((2 * i + core) * share, 128), share)]
        gram[i * share : (i + 1) * share, :] = jnp.dot(left.T, full[...], preferred_element_type=jnp.float32)
    quarter = share // 2

    def block(which, side):
        return gram[pl.ds(pl.multiple_of(which * share + side * quarter, 64), quarter), :]

    near_ref[...] = block(1 - chip, half).astype(jnp.bfloat16)
    side_ref[...] = block(chip, 1 - half).astype(jnp.bfloat16)
    far_ref[...] = block(1 - chip, 1 - half).astype(jnp.bfloat16)
    keep_ref[...] = block(chip, half)


def flip(array, expert_bit, tensor_bits):
    ne, nt = lax.axis_size("expert"), lax.axis_size("tensor")
    route = [
        (e * nt + t, (e ^ expert_bit) * nt + (t ^ tensor_bits)) for e in range(ne) for t in range(nt)
    ]
    return lax.ppermute(array, ("expert", "tensor"), route)


def across(array):
    ne, nt = lax.axis_size("expert"), lax.axis_size("tensor")
    route = []
    for e in range(ne):
        for t in range(nt):
            y_hi = (e % Y_HI + (1 if t // 2 else -1)) % Y_HI
            route.append((e * nt + t, (e // Y_HI * Y_HI + y_hi) * nt + (t ^ 3)))
    return lax.ppermute(array, ("expert", "tensor"), route)


def on_device(acts, hidden_grad, counts, momentum, act_grad):
    n_tensor = lax.axis_size("tensor")
    e = lax.axis_index("expert")
    t = lax.axis_index("tensor")
    sections = lax.axis_size("pipe")
    _, _, rows, half_d = acts.shape
    own_rows, hidden = momentum.shape[2:]
    quarter = PANEL // (2 * n_tensor)

    mine = lax.dynamic_index_in_dim(hidden_grad[0], e // 2, 0, keepdims=False)
    target = e // Y_HI * Y_HI + (e % Y_HI + jnp.where(t // 2 > 0, 1, -1)) % Y_HI
    other = lax.dynamic_index_in_dim(hidden_grad[0], target // 2, 0, keepdims=False)
    h3 = across(other)
    h2 = flip(mine, 0, 2)
    h1 = flip(mine, 0, 1)
    own = momentum[0, 0]
    mate = flip(own, 0, 1)
    received = lax.ppermute(act_grad, "pipe", [(i + 1, i) for i in range(sections - 1)])

    bf16, f32 = jnp.bfloat16, jnp.float32
    vmem = pl.BlockSpec(memory_space=pltpu.VMEM)
    xt = pl.pallas_call(
        prepare,
        out_shape=jax.ShapeDtypeStruct((2 * own_rows, rows), bf16),
        in_specs=[pl.BlockSpec(memory_space=pl.ANY), pl.BlockSpec(memory_space=pltpu.SMEM)],
        out_specs=vmem,
        scratch_shapes=[pltpu.VMEM((rows, 2 * own_rows), bf16), pltpu.SemaphoreType.DMA],
        cost_estimate=pl.CostEstimate(flops=0, bytes_accessed=4 * rows * own_rows * 2, transcendentals=0),
        compiler_params=pltpu.CompilerParams(vmem_limit_bytes=8 << 20),
        name="prepare",
    )(acts, counts)
    block = jax.ShapeDtypeStruct((quarter, hidden), bf16)
    new, keep, near, side, far = pl.pallas_call(
        main,
        out_shape=(
            jax.ShapeDtypeStruct((own_rows, hidden), bf16),
            jax.ShapeDtypeStruct((quarter, hidden), f32),
            block,
            block,
            block,
        ),
        in_specs=[vmem] * 7,
        out_specs=(vmem,) * 5,
        scratch_shapes=[pltpu.VMEM((2 * own_rows, hidden), bf16), pltpu.VMEM((PANEL // 2, hidden), f32)],
        cost_estimate=pl.CostEstimate(
            flops=4 * own_rows * hidden * (rows + PANEL // 2), bytes_accessed=8 * own_rows * hidden, transcendentals=0
        ),
        compiler_params=pltpu.CompilerParams(vmem_limit_bytes=20 << 20),
        name="gradients",
    )(xt, mine, h1, h2, h3, own, mate)
    far = flip(far, 1, 2)
    side = flip(side, 1, 0)
    near = flip(near, 0, 2)
    gram = (keep + near.astype(f32) + side.astype(f32) + far.astype(f32)) / D
    return new[None, None], gram[None, None], received


def solution(mesh):
    return jax.shard_map(
        on_device,
        mesh=mesh,
        in_specs=(
            P("pipe", "expert", None, None),
            P("pipe", None, None, "tensor"),
            P("pipe", None, None),
            P("pipe", "expert", "tensor", None),
            P("pipe", "expert", "tensor"),
        ),
        out_specs=(
            P("pipe", "expert", "tensor", None),
            P("pipe", "expert", "tensor", None),
            P("pipe", "expert", "tensor"),
        ),
        check_vma=False,
    )
```

```python
import jax
import jax.numpy as jnp
from jax import lax
from jax.experimental import pallas as pl
from jax.experimental.pallas import tpu as pltpu
from jax.sharding import PartitionSpec as P


D = 3584
PANEL = 512
Y_HI = 4
DECAY = 0.9


def fetch(grad_ref, acts_ref, mine_ref, other_ref, window_ref, sems):
    t, e = lax.axis_index("tensor"), lax.axis_index("expert")
    width = window_ref.shape[1]
    start = pl.multiple_of(t // 2 * width, 128)
    copies = [
        pltpu.make_async_copy(grad_ref.at[0, e // 2], mine_ref, sems.at[0]),
        pltpu.make_async_copy(grad_ref.at[0, neighbour(e, t) // 2], other_ref, sems.at[1]),
        pltpu.make_async_copy(acts_ref.at[0, 0, :, pl.ds(start, width)], window_ref, sems.at[2]),
    ]
    for copy in copies:
        copy.start()
    for copy in copies:
        copy.wait()


def prepare(window_ref, counts_ref, xt_ref):
    pair = lax.axis_index("expert") // 2
    rows, width = window_ref.shape
    micro = counts_ref.shape[2]
    block = rows // micro
    row = lax.broadcasted_iota(jnp.int32, (block, width), 0)
    for m in range(micro):
        part = window_ref[m * block : (m + 1) * block, :]
        part = jnp.where(row < counts_ref[0, pair, m], part, jnp.zeros_like(part))
        xt_ref[:, m * block : (m + 1) * block] = part.T


def main(xt_ref, h0, h1, h2, h3, own_ref, mate_ref, new_ref, keep_ref, near_ref, side_ref, far_ref, full, gram, sem):
    t = lax.axis_index("tensor")
    half = lax.axis_index("expert") % 2
    core, chip = t % 2, t // 2
    rows = own_ref.shape[0]
    for k, piece in enumerate((h0, h1, h2, h3)):
        width = piece.shape[1]
        col = pl.multiple_of(jnp.bitwise_xor(t, k) * width, 128)
        for i, (who, moment) in enumerate(((core, own_ref), (1 - core, mate_ref))):
            x = xt_ref[pl.ds(pl.multiple_of(who * rows, 64), rows), :]
            grad = jnp.dot(x, piece[...], preferred_element_type=jnp.float32).astype(jnp.bfloat16)
            new = DECAY * moment[:, pl.ds(col, width)].astype(jnp.float32) + grad.astype(jnp.float32)
            new = new.astype(jnp.bfloat16)
            full[i * rows : (i + 1) * rows, pl.ds(col, width)] = new
    store = pltpu.make_async_copy(full.at[pl.ds(0, rows)], new_ref, sem)
    store.start()
    share = gram.shape[0] // 2
    for i in range(2):
        left = full[:, pl.ds(pl.multiple_of((2 * i + core) * share, 128), share)]
        gram[i * share : (i + 1) * share, :] = jnp.dot(left.T, full[...], preferred_element_type=jnp.float32)
    quarter = share // 2

    def block(which, side):
        return gram[pl.ds(pl.multiple_of(which * share + side * quarter, 64), quarter), :]

    near_ref[...] = block(1 - chip, half).astype(jnp.bfloat16)
    side_ref[...] = block(chip, 1 - half).astype(jnp.bfloat16)
    far_ref[...] = block(1 - chip, 1 - half).astype(jnp.bfloat16)
    keep_ref[...] = block(chip, half)
    store.wait()


def finish(keep_ref, near_ref, side_ref, far_ref, arrived_ref, gram_ref, received_ref, sem):
    store = pltpu.make_async_copy(arrived_ref, received_ref, sem)
    store.start()
    total = keep_ref[...] + near_ref[...].astype(jnp.float32)
    total += side_ref[...].astype(jnp.float32) + far_ref[...].astype(jnp.float32)
    gram_ref[...] = total / D
    store.wait()


def neighbour(e, t):
    return e // Y_HI * Y_HI + lax.rem(e % Y_HI + jnp.where(t >= 2, 1, Y_HI - 1), Y_HI)


def flip(array, expert_bit, tensor_bits):
    ne, nt = lax.axis_size("expert"), lax.axis_size("tensor")
    route = [
        (e * nt + t, (e ^ expert_bit) * nt + (t ^ tensor_bits)) for e in range(ne) for t in range(nt)
    ]
    return lax.ppermute(array, ("expert", "tensor"), route)


def across(array):
    ne, nt = lax.axis_size("expert"), lax.axis_size("tensor")
    route = []
    for e in range(ne):
        for t in range(nt):
            y_hi = (e % Y_HI + (1 if t // 2 else -1)) % Y_HI
            route.append((e * nt + t, (e // Y_HI * Y_HI + y_hi) * nt + (t ^ 3)))
    return lax.ppermute(array, ("expert", "tensor"), route)


def on_device(acts, hidden_grad, counts, momentum, act_grad):
    n_tensor = lax.axis_size("tensor")
    sections = lax.axis_size("pipe")
    _, _, rows, _ = acts.shape
    own_rows, hidden = momentum.shape[2:]
    slice_width = hidden_grad.shape[3]
    quarter = PANEL // (2 * n_tensor)
    bf16, f32 = jnp.bfloat16, jnp.float32
    vmem = pl.BlockSpec(memory_space=pltpu.VMEM)
    hbm = pl.BlockSpec(memory_space=pltpu.HBM)
    shape = jax.ShapeDtypeStruct

    mine, other, window = pl.pallas_call(
        fetch,
        out_shape=(shape((rows, slice_width), bf16),) * 2 + (shape((rows, 2 * own_rows), bf16),),
        in_specs=[hbm, hbm],
        out_specs=(vmem,) * 3,
        scratch_shapes=[pltpu.SemaphoreType.DMA((3,))],
        compiler_params=pltpu.CompilerParams(vmem_limit_bytes=8 << 20),
        cost_estimate=pl.CostEstimate(flops=0, bytes_accessed=4 * rows * own_rows * 2, transcendentals=0),
        name="fetch",
    )(pltpu.with_memory_space_constraint(hidden_grad, pltpu.HBM), pltpu.with_memory_space_constraint(acts, pltpu.HBM))
    h2 = flip(mine, 0, 2)
    h3 = across(other)
    own = momentum[0, 0]
    mate = flip(own, 0, 1)
    h1 = flip(mine, 0, 1)
    xt = pl.pallas_call(
        prepare,
        out_shape=shape((2 * own_rows, rows), bf16),
        in_specs=[vmem, pl.BlockSpec(memory_space=pltpu.SMEM)],
        out_specs=vmem,
        compiler_params=pltpu.CompilerParams(vmem_limit_bytes=8 << 20),
        cost_estimate=pl.CostEstimate(flops=0, bytes_accessed=4 * rows * own_rows * 2, transcendentals=0),
        name="prepare",
    )(window, counts)
    block = shape((quarter, hidden), bf16)
    new, keep, near, side, far = pl.pallas_call(
        main,
        out_shape=(shape((own_rows, hidden), bf16), shape((quarter, hidden), f32), block, block, block),
        in_specs=[vmem] * 7,
        out_specs=(hbm,) + (vmem,) * 4,
        scratch_shapes=[
            pltpu.VMEM((2 * own_rows, hidden), bf16),
            pltpu.VMEM((PANEL // 2, hidden), f32),
            pltpu.SemaphoreType.DMA,
        ],
        compiler_params=pltpu.CompilerParams(vmem_limit_bytes=20 << 20),
        cost_estimate=pl.CostEstimate(
            flops=4 * own_rows * hidden * (rows + PANEL // 2),
            bytes_accessed=8 * own_rows * hidden,
            transcendentals=0,
        ),
        name="gradients",
    )(xt, mine, h1, h2, h3, own, mate)
    far = flip(far, 1, 2)
    arrived = lax.ppermute(act_grad[0], "pipe", [(i + 1, i) for i in range(sections - 1)])
    side = flip(side, 1, 0)
    near = flip(near, 0, 2)
    gram, received = pl.pallas_call(
        finish,
        out_shape=(shape((quarter, hidden), f32), shape(arrived.shape, bf16)),
        in_specs=[vmem] * 4 + [pl.BlockSpec(memory_space=pl.ANY)],
        out_specs=(vmem, hbm),
        scratch_shapes=[pltpu.SemaphoreType.DMA],
        compiler_params=pltpu.CompilerParams(vmem_limit_bytes=8 << 20),
        cost_estimate=pl.CostEstimate(flops=0, bytes_accessed=20 * quarter * hidden, transcendentals=0),
        name="finish",
    )(keep, near, side, far, arrived)
    return new[None, None], gram[None, None], received[None]


def solution(mesh):
    return jax.shard_map(
        on_device,
        mesh=mesh,
        in_specs=(
            P("pipe", "expert", None, None),
            P("pipe", None, None, "tensor"),
            P("pipe", None, None),
            P("pipe", "expert", "tensor", None),
            P("pipe", "expert", "tensor"),
        ),
        out_specs=(
            P("pipe", "expert", "tensor", None),
            P("pipe", "expert", "tensor", None),
            P("pipe", "expert", "tensor"),
        ),
        check_vma=False,
    )
```

```python
import jax
import jax.numpy as jnp
from jax import lax
from jax.experimental import pallas as pl
from jax.experimental.pallas import tpu as pltpu
from jax.sharding import PartitionSpec as P


D = 3584
PANEL = 512
Y_HI = 4
DECAY = 0.9


def run_copies(moves, sems):
    copies = [pltpu.make_async_copy(source, target, sems.at[i]) for i, (source, target) in enumerate(moves)]
    for copy in copies:
        copy.start()
    for copy in copies:
        copy.wait()


def fetch(grad_ref, outer_ref, cross_ref, sems):
    t, e = lax.axis_index("tensor"), lax.axis_index("expert")
    run_copies(
        [(grad_ref.at[0, along(e, t) // 2], outer_ref), (grad_ref.at[0, diagonal(e, t) // 2], cross_ref)], sems
    )


def pack(grad_ref, acts_ref, moment_ref, packed_ref, window_ref, sems):
    t, e = lax.axis_index("tensor"), lax.axis_index("expert")
    width = window_ref.shape[1]
    start = pl.multiple_of(t // 2 * width, 128)
    rows = moment_ref.shape[2]
    deep, wide = packed_ref.shape[0] - rows, grad_ref.shape[3]
    moves = [(moment_ref.at[0, 0], packed_ref.at[pl.ds(0, rows)])]
    for k in range(packed_ref.shape[1] // wide):
        moves.append(
            (grad_ref.at[0, e // 2, pl.ds(k * deep, deep)], packed_ref.at[pl.ds(rows, deep), pl.ds(k * wide, wide)])
        )
    moves.append((acts_ref.at[0, 0, :, pl.ds(start, width)], window_ref))
    run_copies(moves, sems)


def prepare(window_ref, counts_ref, xt_ref):
    pair = lax.axis_index("expert") // 2
    rows, width = window_ref.shape
    micro = counts_ref.shape[2]
    block = rows // micro
    row = lax.broadcasted_iota(jnp.int32, (block, width), 0)
    for m in range(micro):
        part = window_ref[m * block : (m + 1) * block, :]
        part = jnp.where(row < counts_ref[0, pair, m], part, jnp.zeros_like(part))
        xt_ref[:, m * block : (m + 1) * block] = part.T


def main(xt_ref, own_ref, h2, h3, mate_ref, new_ref, keep_ref, near_ref, side_ref, far_ref, full, gram, sem):
    t = lax.axis_index("tensor")
    half = lax.axis_index("expert") % 2
    core, chip = t % 2, t // 2
    rows = new_ref.shape[0]
    width = h2.shape[1]
    deep = own_ref.shape[0] - rows
    unpack = lambda ref: jnp.concatenate([ref[rows:, k * width : (k + 1) * width] for k in range(h2.shape[0] // deep)])
    for k, piece in enumerate((unpack(own_ref), unpack(mate_ref), h2[...], h3[...])):
        col = pl.multiple_of(jnp.bitwise_xor(t, k) * width, 128)
        for i, (who, moment) in enumerate(((core, own_ref), (1 - core, mate_ref))):
            x = xt_ref[pl.ds(pl.multiple_of(who * rows, 64), rows), :]
            grad = jnp.dot(x, piece, preferred_element_type=jnp.float32).astype(jnp.bfloat16)
            new = DECAY * moment[:rows, pl.ds(col, width)].astype(jnp.float32) + grad.astype(jnp.float32)
            full[i * rows : (i + 1) * rows, pl.ds(col, width)] = new.astype(jnp.bfloat16)
    store = pltpu.make_async_copy(full.at[pl.ds(0, rows)], new_ref, sem)
    store.start()
    share = gram.shape[0] // 2
    left = [full[:, pl.ds(pl.multiple_of((2 * i + core) * share, 128), share)].T for i in range(2)]
    gram[...] = jnp.dot(jnp.concatenate(left), full[...], preferred_element_type=jnp.float32)
    quarter = share // 2

    def block(which, side):
        return gram[pl.ds(pl.multiple_of(which * share + side * quarter, 64), quarter), :]

    near_ref[...] = block(1 - chip, half).astype(jnp.bfloat16)
    side_ref[...] = block(chip, 1 - half).astype(jnp.bfloat16)
    far_ref[...] = block(1 - chip, 1 - half).astype(jnp.bfloat16)
    keep_ref[...] = block(chip, half)
    store.wait()


def finish(keep_ref, near_ref, side_ref, far_ref, arrived_ref, gram_ref, received_ref, total_ref, sems):
    relay = pltpu.make_async_copy(arrived_ref, received_ref, sems.at[0])
    relay.start()
    total = keep_ref[...] + near_ref[...].astype(jnp.float32)
    total += side_ref[...].astype(jnp.float32) + far_ref[...].astype(jnp.float32)
    total_ref[...] = total / D
    store = pltpu.make_async_copy(total_ref, gram_ref, sems.at[1])
    store.start()
    relay.wait()
    store.wait()


def along(e, t):
    return e // Y_HI * Y_HI + (e % Y_HI + (t // 2 * 2 - 1) + Y_HI) % Y_HI


def diagonal(e, t):
    count = lax.axis_size("expert")
    return (e + (t // 2 * 2 - 1) * Y_HI + count) % count


def flip(array, expert_bit, tensor_bits):
    ne, nt = lax.axis_size("expert"), lax.axis_size("tensor")
    route = [
        (e * nt + t, (e ^ expert_bit) * nt + (t ^ tensor_bits)) for e in range(ne) for t in range(nt)
    ]
    return lax.ppermute(array, ("expert", "tensor"), route)


def exchange(array, partner, flipped):
    ne, nt = lax.axis_size("expert"), lax.axis_size("tensor")
    route = [(e * nt + t, partner(e, t) * nt + (t ^ flipped)) for e in range(ne) for t in range(nt)]
    return lax.ppermute(array, ("expert", "tensor"), route)


def on_device(acts, hidden_grad, counts, momentum, act_grad):
    n_tensor = lax.axis_size("tensor")
    sections = lax.axis_size("pipe")
    _, _, rows, _ = acts.shape
    own_rows, hidden = momentum.shape[2:]
    slice_width = hidden_grad.shape[3]
    quarter = PANEL // (2 * n_tensor)
    bf16, f32 = jnp.bfloat16, jnp.float32
    vmem = pl.BlockSpec(memory_space=pltpu.VMEM)
    hbm = pl.BlockSpec(memory_space=pltpu.HBM)
    shape = jax.ShapeDtypeStruct

    in_hbm = lambda array: pltpu.with_memory_space_constraint(array, pltpu.HBM)
    deep = rows * slice_width // hidden
    in_hbm = lambda array: pltpu.with_memory_space_constraint(array, pltpu.HBM)
    deep = rows * slice_width // hidden
    piece = shape((rows, slice_width), bf16)
    outer, cross = pl.pallas_call(
        fetch,
        out_shape=(piece, piece),
        in_specs=[hbm],
        out_specs=(vmem,) * 2,
        scratch_shapes=[pltpu.SemaphoreType.DMA((2,))],
        compiler_params=pltpu.CompilerParams(vmem_limit_bytes=8 << 20),
        cost_estimate=pl.CostEstimate(flops=0, bytes_accessed=8 * rows * slice_width, transcendentals=0),
        name="fetch",
    )(in_hbm(hidden_grad))
    h2 = exchange(outer, along, 2)
    h3 = exchange(cross, diagonal, 3)
    own, window = pl.pallas_call(
        pack,
        out_shape=(shape((own_rows + deep, hidden), bf16), shape((rows, 2 * own_rows), bf16)),
        in_specs=[hbm] * 3,
        out_specs=(vmem,) * 2,
        scratch_shapes=[pltpu.SemaphoreType.DMA((2 + rows // deep,))],
        compiler_params=pltpu.CompilerParams(vmem_limit_bytes=8 << 20),
        cost_estimate=pl.CostEstimate(flops=0, bytes_accessed=8 * rows * own_rows * 2, transcendentals=0),
        name="pack",
    )(in_hbm(hidden_grad), in_hbm(acts), in_hbm(momentum))
    mate = flip(own, 0, 1)
    arrived = lax.ppermute(act_grad[0], "pipe", [(i + 1, i) for i in range(sections - 1)])
    xt = pl.pallas_call(
        prepare,
        out_shape=shape((2 * own_rows, rows), bf16),
        in_specs=[vmem, pl.BlockSpec(memory_space=pltpu.SMEM)],
        out_specs=vmem,
        compiler_params=pltpu.CompilerParams(vmem_limit_bytes=8 << 20),
        cost_estimate=pl.CostEstimate(flops=0, bytes_accessed=4 * rows * own_rows * 2, transcendentals=0),
        name="prepare",
    )(window, counts)
    block = shape((quarter, hidden), bf16)
    new, keep, near, side, far = pl.pallas_call(
        main,
        out_shape=(shape((own_rows, hidden), bf16), shape((quarter, hidden), f32), block, block, block),
        in_specs=[vmem] * 5,
        out_specs=(hbm,) + (vmem,) * 4,
        scratch_shapes=[
            pltpu.VMEM((2 * own_rows, hidden), bf16),
            pltpu.VMEM((PANEL // 2, hidden), f32),
            pltpu.SemaphoreType.DMA,
        ],
        compiler_params=pltpu.CompilerParams(vmem_limit_bytes=20 << 20),
        cost_estimate=pl.CostEstimate(
            flops=4 * own_rows * hidden * (rows + PANEL // 2),
            bytes_accessed=8 * own_rows * hidden,
            transcendentals=0,
        ),
        name="gradients",
    )(xt, own, h2, h3, mate)
    far = flip(far, 1, 2)
    side = flip(side, 1, 0)
    near = flip(near, 0, 2)
    gram, received = pl.pallas_call(
        finish,
        out_shape=(shape((quarter, hidden), f32), shape(arrived.shape, bf16)),
        in_specs=[vmem] * 4 + [pl.BlockSpec(memory_space=pl.ANY)],
        out_specs=(hbm, hbm),
        scratch_shapes=[pltpu.VMEM((quarter, hidden), f32), pltpu.SemaphoreType.DMA((2,))],
        compiler_params=pltpu.CompilerParams(vmem_limit_bytes=8 << 20),
        cost_estimate=pl.CostEstimate(flops=0, bytes_accessed=20 * quarter * hidden, transcendentals=0),
        name="finish",
    )(keep, near, side, far, arrived)
    return new[None, None], gram[None, None], received[None]


def solution(mesh):
    return jax.shard_map(
        on_device,
        mesh=mesh,
        in_specs=(
            P("pipe", "expert", None, None),
            P("pipe", None, None, "tensor"),
            P("pipe", None, None),
            P("pipe", "expert", "tensor", None),
            P("pipe", "expert", "tensor"),
        ),
        out_specs=(
            P("pipe", "expert", "tensor", None),
            P("pipe", "expert", "tensor", None),
            P("pipe", "expert", "tensor"),
        ),
        check_vma=False,
    )
```

```python
import jax
import jax.numpy as jnp
from jax import lax
from jax.experimental import pallas as pl
from jax.experimental.pallas import tpu as pltpu
from jax.sharding import PartitionSpec as P


D = 3584
PANEL = 512
Y_HI = 4
DECAY = 0.9


def fetch(grad_ref, acts_ref, moment_ref, packed_ref, outer_ref, cross_ref, window_ref, sems):
    t, e = lax.axis_index("tensor"), lax.axis_index("expert")
    width = window_ref.shape[1]
    start = pl.multiple_of(t // 2 * width, 128)
    rows = moment_ref.shape[2]
    deep, wide = packed_ref.shape[0] - rows, grad_ref.shape[3]
    moves = [
        (grad_ref.at[0, (e ^ Y_HI) // 2], cross_ref),
        (grad_ref.at[0, along(e, t) // 2], outer_ref),
        (moment_ref.at[0, 0], packed_ref.at[pl.ds(0, rows)]),
    ]
    for k in range(packed_ref.shape[1] // wide):
        moves.append(
            (grad_ref.at[0, e // 2, pl.ds(k * deep, deep)], packed_ref.at[pl.ds(rows, deep), pl.ds(k * wide, wide)])
        )
    moves.append((acts_ref.at[0, 0, :, pl.ds(start, width)], window_ref))
    copies = [pltpu.make_async_copy(a, b, sems.at[i]) for i, (a, b) in enumerate(moves)]
    for copy in copies:
        copy.start()
    for copy in copies:
        copy.wait()


def prepare(window_ref, counts_ref, xt_ref):
    pair = lax.axis_index("expert") // 2
    rows, width = window_ref.shape
    micro = counts_ref.shape[2]
    block = rows // micro
    row = lax.broadcasted_iota(jnp.int32, (block, width), 0)
    for m in range(micro):
        part = window_ref[m * block : (m + 1) * block, :]
        part = jnp.where(row < counts_ref[0, pair, m], part, jnp.zeros_like(part))
        xt_ref[:, m * block : (m + 1) * block] = part.T


def main(xt_ref, own_ref, h2, h3, mate_ref, new_ref, keep_ref, near_ref, side_ref, far_ref, full, gram, sem):
    t = lax.axis_index("tensor")
    half = lax.axis_index("expert") % 2
    core, chip = t % 2, t // 2
    rows = new_ref.shape[0]
    width = h2.shape[1]
    deep = own_ref.shape[0] - rows
    unpack = lambda ref: jnp.concatenate([ref[rows:, k * width : (k + 1) * width] for k in range(h2.shape[0] // deep)])
    for k, piece in enumerate((unpack(own_ref), unpack(mate_ref), h2[...], h3[...])):
        col = pl.multiple_of(jnp.bitwise_xor(t, k) * width, 128)
        for i, (who, moment) in enumerate(((core, own_ref), (1 - core, mate_ref))):
            x = xt_ref[pl.ds(pl.multiple_of(who * rows, 64), rows), :]
            grad = jnp.dot(x, piece, preferred_element_type=jnp.float32).astype(jnp.bfloat16)
            new = DECAY * moment[:rows, pl.ds(col, width)].astype(jnp.float32) + grad.astype(jnp.float32)
            full[i * rows : (i + 1) * rows, pl.ds(col, width)] = new.astype(jnp.bfloat16)
    store = pltpu.make_async_copy(full.at[pl.ds(0, rows)], new_ref, sem)
    store.start()
    share = gram.shape[0] // 2
    left = [full[:, pl.ds(pl.multiple_of((2 * i + core) * share, 128), share)].T for i in range(2)]
    gram[...] = jnp.dot(jnp.concatenate(left), full[...], preferred_element_type=jnp.float32)
    quarter = share // 2

    def block(which, side):
        return gram[pl.ds(pl.multiple_of(which * share + side * quarter, 64), quarter), :]

    near_ref[...] = block(1 - chip, half).astype(jnp.bfloat16)
    side_ref[...] = block(chip, 1 - half).astype(jnp.bfloat16)
    far_ref[...] = block(1 - chip, 1 - half).astype(jnp.bfloat16)
    keep_ref[...] = block(chip, half)
    store.wait()


def finish(keep_ref, near_ref, side_ref, far_ref, arrived_ref, gram_ref, received_ref, total_ref, sems):
    relay = pltpu.make_async_copy(arrived_ref, received_ref, sems.at[0])
    relay.start()
    total = keep_ref[...] + near_ref[...].astype(jnp.float32)
    total += side_ref[...].astype(jnp.float32) + far_ref[...].astype(jnp.float32)
    total_ref[...] = total / D
    store = pltpu.make_async_copy(total_ref, gram_ref, sems.at[1])
    store.start()
    relay.wait()
    store.wait()


def along(e, t):
    return e // Y_HI * Y_HI + (e % Y_HI + (t // 2 * 2 - 1) + Y_HI) % Y_HI


def flip(array, expert_bit, tensor_bits):
    ne, nt = lax.axis_size("expert"), lax.axis_size("tensor")
    route = [
        (e * nt + t, (e ^ expert_bit) * nt + (t ^ tensor_bits)) for e in range(ne) for t in range(nt)
    ]
    return lax.ppermute(array, ("expert", "tensor"), route)


def exchange(array, partner, flipped):
    ne, nt = lax.axis_size("expert"), lax.axis_size("tensor")
    route = [(e * nt + t, partner(e, t) * nt + (t ^ flipped)) for e in range(ne) for t in range(nt)]
    return lax.ppermute(array, ("expert", "tensor"), route)


def on_device(acts, hidden_grad, counts, momentum, act_grad):
    n_tensor = lax.axis_size("tensor")
    sections = lax.axis_size("pipe")
    _, _, rows, _ = acts.shape
    own_rows, hidden = momentum.shape[2:]
    slice_width = hidden_grad.shape[3]
    quarter = PANEL // (2 * n_tensor)
    bf16, f32 = jnp.bfloat16, jnp.float32
    vmem = pl.BlockSpec(memory_space=pltpu.VMEM)
    hbm = pl.BlockSpec(memory_space=pltpu.HBM)
    shape = jax.ShapeDtypeStruct

    in_hbm = lambda array: pltpu.with_memory_space_constraint(array, pltpu.HBM)
    deep = rows * slice_width // hidden
    own, outer, cross, window = pl.pallas_call(
        fetch,
        out_shape=(
            shape((own_rows + deep, hidden), bf16),
            shape((rows, slice_width), bf16),
            shape((rows, slice_width), bf16),
            shape((rows, 2 * own_rows), bf16),
        ),
        in_specs=[hbm] * 3,
        out_specs=(vmem,) * 4,
        scratch_shapes=[pltpu.SemaphoreType.DMA((4 + rows // deep,))],
        compiler_params=pltpu.CompilerParams(vmem_limit_bytes=8 << 20),
        cost_estimate=pl.CostEstimate(flops=0, bytes_accessed=8 * rows * own_rows * 2, transcendentals=0),
        name="fetch",
    )(in_hbm(hidden_grad), in_hbm(acts), in_hbm(momentum))
    h3 = flip(cross, Y_HI, 3)
    h2 = exchange(outer, along, 2)
    mate = flip(own, 0, 1)
    arrived = lax.ppermute(act_grad[0], "pipe", [(i + 1, i) for i in range(sections - 1)])
    xt = pl.pallas_call(
        prepare,
        out_shape=shape((2 * own_rows, rows), bf16),
        in_specs=[vmem, pl.BlockSpec(memory_space=pltpu.SMEM)],
        out_specs=vmem,
        compiler_params=pltpu.CompilerParams(vmem_limit_bytes=8 << 20),
        cost_estimate=pl.CostEstimate(flops=0, bytes_accessed=4 * rows * own_rows * 2, transcendentals=0),
        name="prepare",
    )(window, counts)
    block = shape((quarter, hidden), bf16)
    new, keep, near, side, far = pl.pallas_call(
        main,
        out_shape=(shape((own_rows, hidden), bf16), shape((quarter, hidden), f32), block, block, block),
        in_specs=[vmem] * 5,
        out_specs=(hbm,) + (vmem,) * 4,
        scratch_shapes=[
            pltpu.VMEM((2 * own_rows, hidden), bf16),
            pltpu.VMEM((PANEL // 2, hidden), f32),
            pltpu.SemaphoreType.DMA,
        ],
        compiler_params=pltpu.CompilerParams(vmem_limit_bytes=20 << 20),
        cost_estimate=pl.CostEstimate(
            flops=4 * own_rows * hidden * (rows + PANEL // 2),
            bytes_accessed=8 * own_rows * hidden,
            transcendentals=0,
        ),
        name="gradients",
    )(xt, own, h2, h3, mate)
    far = flip(far, 1, 2)
    side = flip(side, 1, 0)
    near = flip(near, 0, 2)
    gram, received = pl.pallas_call(
        finish,
        out_shape=(shape((quarter, hidden), f32), shape(arrived.shape, bf16)),
        in_specs=[vmem] * 4 + [pl.BlockSpec(memory_space=pl.ANY)],
        out_specs=(hbm, hbm),
        scratch_shapes=[pltpu.VMEM((quarter, hidden), f32), pltpu.SemaphoreType.DMA((2,))],
        compiler_params=pltpu.CompilerParams(vmem_limit_bytes=8 << 20),
        cost_estimate=pl.CostEstimate(flops=0, bytes_accessed=20 * quarter * hidden, transcendentals=0),
        name="finish",
    )(keep, near, side, far, arrived)
    return new[None, None], gram[None, None], received[None]


def solution(mesh):
    return jax.shard_map(
        on_device,
        mesh=mesh,
        in_specs=(
            P("pipe", "expert", None, None),
            P("pipe", None, None, "tensor"),
            P("pipe", None, None),
            P("pipe", "expert", "tensor", None),
            P("pipe", "expert", "tensor"),
        ),
        out_specs=(
            P("pipe", "expert", "tensor", None),
            P("pipe", "expert", "tensor", None),
            P("pipe", "expert", "tensor"),
        ),
        check_vma=False,
    )
```
